1024 devices in a mesh: gz: 64 (over x_lo, y, core), xy: 16 (over x_hi, z).
Axes of the slice: x: 8 (x_hi: 2, x_lo: 4; x = x_hi * 4 + x_lo), y: 8, z: 8, core: 2. Of those that a mesh axis runs over, the one named last changes fastest.
Arguments:
- flux_xface: bfloat16 [64, 2048, 2048], P(None, 'gz', 'xy'), may hold values from -6 to 6
- flux_yspec: bfloat16 [64, 2048, 2048], P(None, 'gz', 'xy'), may hold values from -6 to 6
- flux_zface: bfloat16 [64, 2048, 2048], P(None, 'gz', 'xy'), may hold values from -6 to 6
- frequency_y: int32 [64], replicated, may hold values from 0 to 2047
Outputs:
- potential: float32 [64, 2048, 2, 1024], P('gz', 'xy')
The draws below stay inside these ranges and needn't reach their ends.
All inputs are finite; a program needn't handle non-finite values.
Results may differ from the reference program's by a relative error of at most 0.0003.
Values may be sent and summed in bfloat16 or wider, within the bound.
A program may use at most 32 MiB of HBM per device.

```python
import math
import jax
import jax.numpy as jnp
from jax import lax

NX = 2048
NY = 2048
NZ = 2048
YW = 64


def touch_ends(result, key, least, high):
    extent = result.shape
    spot = [jax.random.randint(jax.random.fold_in(key, axis), (), 0, extent[axis]) for axis in range(len(extent))]
    result = result.at[tuple(spot)].set(least)
    longest = extent.index(max(extent))
    spot[longest] = (spot[longest] + 1) % extent[longest]
    return result.at[tuple(spot)].set(high)


def levels(stream_key, shape, cuts, low, high):
    def one(axis_at, blocks):
        draws = jax.random.uniform(jax.random.fold_in(jax.random.fold_in(stream_key, 6), axis_at), (blocks,), jnp.float32, low / len(cuts), high / len(cuts))
        return jnp.repeat(jnp.exp(draws), shape[axis_at] // blocks).reshape((-1,) + (1,) * (len(shape) - axis_at - 1))

    factor_of = one(*cuts[0])
    for cut in cuts[1:]:
        factor_of = factor_of * one(*cut)
    return factor_of


def gaussian(own_key, extent, deviation, most, pieces=(), held_as=jnp.bfloat16):
    values = jax.random.normal(own_key, extent, jnp.float32) * deviation
    if len(pieces) > 0:
        values = levels(own_key, extent, pieces, -0.22, 0.18) * values
    return jnp.clip(values, min=-most, max=most).astype(held_as)


def setup_inputs(seed: int = 0) -> dict:
    key_list = jax.random.split(jax.random.key(seed), 5)
    flux_xface = gaussian(key_list[0], (YW, NZ, NX), 1.0, 6.0, ((1, 64), (2, 16)))
    flux_yspec = gaussian(key_list[1], (YW, NZ, NX), 1.0, 6.0, ((1, 64), (2, 16)))
    flux_zface = gaussian(key_list[2], (YW, NZ, NX), 1.0, 6.0, ((1, 64), (2, 16)))
    frequency_y = touch_ends(jax.random.randint(key_list[3], (YW,), 0, NY), jax.random.fold_in(key_list[3], 1), 0, NY - 1).astype(jnp.int32)
    return {"flux_xface": flux_xface, "flux_yspec": flux_yspec, "flux_zface": flux_zface, "frequency_y": frequency_y}


SCREEN_WEIGHT = 0.5

def cosine_transform(source, axis):
    moved = jnp.moveaxis(source, axis, -1)
    length = moved.shape[-1]
    reordered = jnp.concatenate([moved[..., 0::2], moved[..., 1::2][..., ::-1]], axis=-1)
    spectral = jnp.fft.fft(reordered, axis=-1)
    index_k = jnp.arange(length, dtype=jnp.int32)
    angle_k = math.pi / (2 * length) * index_k.astype(moved.dtype)
    real_part = jnp.cos(angle_k) * spectral.real + jnp.sin(angle_k) * spectral.imag
    scaling = jnp.where(index_k == 0, math.sqrt(1.0 / length), math.sqrt(2.0 / length)).astype(moved.dtype)
    return jnp.moveaxis(real_part * scaling, -1, axis)

def eigenvalue(length, dtype):
    sine = jnp.sin(jnp.arange(length, dtype=jnp.int32).astype(dtype) * (math.pi / (2 * length)))
    return 4.0 * sine * sine

def one_row(inputs):
    flux_x, flux_y, flux_z, frequency = inputs
    keep_x = (jnp.arange(NX, dtype=jnp.int32) < NX - 1).astype(jnp.float32)
    keep_z = (jnp.arange(NZ, dtype=jnp.int32) < NZ - 1).astype(jnp.float32)
    masked_x = flux_x.astype(jnp.float32) * keep_x[None, :]
    masked_z = flux_z.astype(jnp.float32) * keep_z[:, None]
    diff_x = masked_x - jnp.concatenate([jnp.zeros((NZ, 1), jnp.float32), masked_x[:, :-1]], axis=1)
    diff_z = masked_z - jnp.concatenate([jnp.zeros((1, NX), jnp.float32), masked_z[:-1]], axis=0)
    weight = 2.0 * jnp.sin(frequency.astype(jnp.float32) * (math.pi / (2 * NY)))
    divergence = diff_x + diff_z + weight * flux_y.astype(jnp.float32)
    spectrum = cosine_transform(cosine_transform(divergence, 0), 1)
    lam_z = eigenvalue(NZ, jnp.float32)
    lam_x = eigenvalue(NX, jnp.float32)
    denominator = weight * weight + lam_z[:, None] + lam_x[None, :] + SCREEN_WEIGHT
    potential = -spectrum / denominator
    return jnp.transpose(potential.reshape(NZ, NX // 2, 2), (0, 2, 1))

def reference(flux_xface, flux_yspec, flux_zface, frequency_y):
    return lax.map(one_row, (flux_xface, flux_yspec, flux_zface, frequency_y))
```

```python
import functools
import math

import jax
import jax.numpy as jnp
import numpy as np
from jax import lax
from jax.experimental import pallas as pl
from jax.experimental.pallas import tpu as pltpu
from jax.sharding import PartitionSpec as P

NY = 2048
SCREEN_WEIGHT = 0.5
MESH = pl.DeviceIdType.MESH
LANES = 128
ROWS = 16
STRIDE = 27
CODE_MAX = 32767.0
TINY = 1e-30


def seed_tables(half):
    period = 8 * half
    unit = 2.0 * np.pi / period
    row = np.arange(ROWS)[:, None]
    lane = np.arange(LANES)[None, :]
    phases = []
    for p in range(2):
        phases.append((2 * row + p) * (2 * lane + 1))
    block = np.arange(half // ROWS)[:, None]
    phases.append(2 * ROWS * block * (2 * lane + 1))
    for p in range(2):
        for a in range(half // LANES):
            phases.append((2 * row + p) * (2 * LANES * a) + 0 * lane)
    phase = np.concatenate(phases, axis=0) % period
    return np.stack([np.cos(phase * unit), np.sin(phase * unit)]).astype(np.float32)


def small_sine(angle):
    square = angle * angle
    total = jnp.full_like(angle, 1.0 / 6227020800.0)
    for divisor in (-39916800.0, 362880.0, -5040.0, 120.0, -6.0, 1.0):
        total = total * square + 1.0 / divisor
    return total * angle


def split(value):
    high = value.astype(jnp.bfloat16)
    return high, (value - high.astype(jnp.float32)).astype(jnp.bfloat16)


def coded(value, axis):
    largest = jnp.maximum(jnp.max(jnp.abs(value), axis=axis, keepdims=True), TINY)
    codes = jnp.round(value * (CODE_MAX / largest)).astype(jnp.int32)
    return codes.astype(jnp.int16), largest * (1.0 / CODE_MAX)


def mixed(a, b, transposed=False):
    dims = (((1,), (1,)), ((), ())) if transposed else (((1,), (0,)), ((), ()))
    return lax.dot_general(a, b, dims, preferred_element_type=jnp.float32)


def kernel(
    gz, xy, chunks, w_ref, edge_ref, seed_ref, fx_ref, fy_ref, fz_ref, out_ref,
    fx, fy, fz, seeds, x_edge, code1, side1, got1, gotside1, table_hi, table_lo, planes,
    even, odd, code2, side2, got2, gotside2, lines, even_x, odd_x, factor,
    load_sem, edge_sem, sem1, sem2,
):
    g = lax.axis_index("gz")
    r = lax.axis_index("xy")
    depth = fx_ref.shape[1]
    nz = gz * depth
    half = nz // 2
    turn = min(256, half)
    f32 = jnp.float32

    loads = [
        pltpu.make_async_copy(src, dst, load_sem.at[i])
        for i, (src, dst) in enumerate(((fx_ref, fx), (fz_ref, fz), (fy_ref, fy), (seed_ref, seeds)))
    ]
    for load in loads:
        load.start()

    barrier = pltpu.get_barrier_semaphore()

    @pl.loop(1, gz)
    def _(i):
        pl.semaphore_signal(barrier, inc=1, device_id={"gz": lax.rem(g + i, gz)}, device_id_type=MESH)

    @pl.loop(1, xy)
    def _(i):
        pl.semaphore_signal(barrier, inc=1, device_id={"xy": lax.rem(r + i, xy)}, device_id_type=MESH)

    pl.semaphore_wait(barrier, gz + xy - 2)

    edge_copy = pltpu.make_async_remote_copy(
        src_ref=edge_ref, dst_ref=x_edge, send_sem=edge_sem.at[0], recv_sem=edge_sem.at[1],
        device_id={"xy": lax.rem(r + 1, xy)}, device_id_type=MESH,
    )

    @pl.when(r < xy - 1)
    def _():
        edge_copy.start()

    @pl.when(r == 0)
    def _():
        x_edge[...] = jnp.zeros_like(x_edge)

    for load in loads:
        load.wait()

    @pl.when(r > 0)
    def _():
        edge_copy.wait_recv()

    lane = lax.broadcasted_iota(jnp.int32, (depth, LANES), 1)
    plane = lax.broadcasted_iota(jnp.int32, (depth, LANES), 0)
    x_kept = (lane < LANES - 1) | (r < xy - 1)
    z_kept = (plane < depth - 1) | (g < gz - 1)
    edges = x_edge[...].astype(f32)

    @pl.loop(0, gz, unroll=4)
    def _(y):
        masked_x = jnp.where(x_kept, fx[y].astype(f32), 0.0)
        masked_z = jnp.where(z_kept, fz[y].astype(f32), 0.0)
        before = pltpu.roll(edges, lax.rem(LANES - y, LANES), 1)
        x_before = jnp.where(lane == 0, before, pltpu.roll(masked_x, 1, 1))
        z_before = jnp.where(plane == 0, 0.0, pltpu.roll(masked_z, 1, 0))
        slab = masked_x - x_before + w_ref[y] * fy[y].astype(f32) + masked_z - z_before
        codes, scale = coded(slab, 0)
        code1[y] = codes
        side1[y, :, :LANES] = scale
        side1[y, :, LANES:] = masked_z[depth - 1 :, :]

    def exchange1(peer):
        return (
            pltpu.make_async_remote_copy(
                src_ref=code1.at[peer], dst_ref=got1.at[g], send_sem=sem1.at[0], recv_sem=sem1.at[1],
                device_id={"gz": peer}, device_id_type=MESH,
            ),
            pltpu.make_async_remote_copy(
                src_ref=side1.at[peer], dst_ref=gotside1.at[g], send_sem=sem1.at[2], recv_sem=sem1.at[3],
                device_id={"gz": peer}, device_id_type=MESH,
            ),
        )

    @pl.loop(1, gz)
    def _(i):
        for copy in exchange1(lax.rem(g + i * STRIDE, gz)):
            copy.start()

    got1[g] = code1[g]
    gotside1[g] = side1[g]

    blocks = half // ROWS
    columns = half // LANES

    @pl.loop(0, blocks)
    def _(c):
        step_c = seeds[0, pl.ds(2 * ROWS + c, 1), :]
        step_s = seeds[1, pl.ds(2 * ROWS + c, 1), :]
        top = pl.multiple_of(c * ROWS, ROWS)
        for p in range(2):
            base_c = seeds[0, p * ROWS : (p + 1) * ROWS, :]
            base_s = seeds[1, p * ROWS : (p + 1) * ROWS, :]
            low_c = base_c * step_c - base_s * step_s
            low_s = base_s * step_c + base_c * step_s
            for a in range(columns):
                at = 2 * ROWS + blocks + (p * columns + a) * ROWS
                entry = seeds[0, at : at + ROWS, :] * low_c - seeds[1, at : at + ROWS, :] * low_s
                high, low = split(entry)
                table_hi[p, pl.ds(top, ROWS), a * LANES : (a + 1) * LANES] = high
                table_lo[p, pl.ds(top, ROWS), a * LANES : (a + 1) * LANES] = low

    across = lax.broadcasted_iota(jnp.int32, (turn, turn), 0) + lax.broadcasted_iota(jnp.int32, (turn, turn), 1)
    mirror = jnp.where(across == turn - 1, 1.0, 0.0).astype(jnp.bfloat16)

    def all_but_one(ref, sem):
        part = ref.at[pl.ds(0, ref.shape[0] - 1)]
        return pltpu.make_async_copy(part, part, sem)

    all_but_one(got1, sem1.at[1]).wait()
    all_but_one(gotside1, sem1.at[3]).wait()

    @pl.loop(0, gz, unroll=2)
    def _(k):
        value = got1[k].astype(jnp.int32).astype(f32) * gotside1[k, :, :LANES]
        below = gotside1[jnp.maximum(k - 1, 0), :, LANES:]
        value = value - jnp.where((plane == 0) & (k > 0), below, 0.0)
        high, low = split(value)
        at = pl.ds(pl.multiple_of(k * depth, depth), depth)
        planes[at, :LANES] = high
        planes[at, LANES:] = low

    for b in range(half // turn):
        here = slice(b * turn, (b + 1) * turn)
        there = slice(nz - (b + 1) * turn, nz - b * turn)
        lower = mixed(mirror, planes[there, :])
        lower = lower[:, :LANES] + lower[:, LANES:]
        upper = planes[here, :LANES].astype(f32) + planes[here, LANES:].astype(f32)
        even[here, :LANES], even[here, LANES:] = split(upper + lower)
        odd[here, :LANES], odd[here, LANES:] = split(upper - lower)

    def exchange2(peer):
        return (
            pltpu.make_async_remote_copy(
                src_ref=code2.at[peer], dst_ref=got2.at[r], send_sem=sem2.at[0], recv_sem=sem2.at[1],
                device_id={"xy": peer}, device_id_type=MESH,
            ),
            pltpu.make_async_remote_copy(
                src_ref=side2.at[peer], dst_ref=gotside2.at[r], send_sem=sem2.at[2], recv_sem=sem2.at[3],
                device_id={"xy": peer}, device_id_type=MESH,
            ),
        )

    chunk = half // chunks
    group = xy // chunks
    rows = half // xy

    @pl.loop(0, chunks)
    def _(c):
        at_chunk = lax.rem(r // group + chunks // 2 + c, chunks)
        here = pl.ds(pl.multiple_of(at_chunk * chunk, chunk), chunk)
        parts = []
        for p, folded in enumerate((even, odd)):
            wide = mixed(table_hi[p, here, :], folded[...])
            narrow = mixed(table_lo[p, here, :], folded[:, :LANES])
            parts.append(wide[:, :LANES] + wide[:, LANES:] + narrow)
        for j in range(group):
            peer = at_chunk * group + j
            block = jnp.concatenate([part[j * rows : (j + 1) * rows] for part in parts], axis=0)
            codes, scale = coded(block, 0)
            code2[peer] = codes
            side2[peer] = scale

            @pl.when(peer != r)
            def _():
                for copy in exchange2(peer):
                    copy.start()

    got2[r] = code2[r]
    gotside2[r] = side2[r]

    unit = math.pi / (2 * nz)
    at_row = lax.broadcasted_iota(jnp.int32, (2 * rows, LANES), 0)
    kz = 2 * rows * r + 2 * lax.rem(at_row, rows) + at_row // rows
    sine = small_sine(kz.astype(f32) * unit)
    weight = w_ref[g]
    base = 4.0 * sine * sine + weight * weight + SCREEN_WEIGHT
    gain = jnp.where(kz == 0, -math.sqrt(0.5), -1.0) * (2.0 / nz)
    for p in range(2):
        for a in range(columns):
            kx = 2 * (lax.broadcasted_iota(jnp.int32, (1, LANES), 1) + a * LANES) + p
            sine = small_sine(kx.astype(f32) * unit)
            own = jnp.where(kx == 0, math.sqrt(0.5), 1.0)
            at = (p * columns + a) * LANES
            factor[:, at : at + LANES] = gain * own / (base + 4.0 * sine * sine)

    all_but_one(got2, sem2.at[1]).wait()
    all_but_one(gotside2, sem2.at[3]).wait()

    tall = 2 * rows
    for k in range(xy):
        value = got2[k].astype(jnp.int32).astype(f32) * gotside2[k]
        high, low = split(value)
        lines[:tall, k * LANES : (k + 1) * LANES] = high
        lines[tall:, k * LANES : (k + 1) * LANES] = low

    for b in range(half // turn):
        here = slice(b * turn, (b + 1) * turn)
        there = slice(nz - (b + 1) * turn, nz - b * turn)
        lower = mixed(lines[:, there], mirror)
        lower = lower[:tall] + lower[tall:]
        upper = lines[:tall, here].astype(f32) + lines[tall:, here].astype(f32)
        even_x[:tall, here], even_x[tall:, here] = split(upper + lower)
        odd_x[:tall, here], odd_x[tall:, here] = split(upper - lower)

    for p, folded in enumerate((even_x, odd_x)):
        for b in range(half // turn):
            here = slice(b * turn, (b + 1) * turn)
            wide = mixed(folded[...], table_hi[p, here, :], True)
            narrow = mixed(folded[:tall, :], table_lo[p, here, :], True)
            at = p * half + b * turn
            total = wide[:tall] + wide[tall:] + narrow
            out_ref[:, at : at + turn] = total * factor[:, at : at + turn]

    @pl.when(r < xy - 1)
    def _():
        edge_copy.wait_send()

    for ref, sem in ((code1, sem1.at[0]), (side1, sem1.at[2]), (code2, sem2.at[0]), (side2, sem2.at[2])):
        all_but_one(ref, sem).wait()


def shards(gz, xy, flux_xface, flux_yspec, flux_zface, frequency_y):
    rows_y, depth, width = flux_xface.shape
    nz = gz * depth
    half = nz // 2
    tall = nz // xy
    chunks = 4 if xy >= 8 else 2
    weight_y = 2.0 * jnp.sin(frequency_y.astype(jnp.float32) * (math.pi / (2 * NY)))
    weight = jnp.broadcast_to(weight_y[:, None, None], (rows_y, 1, LANES))
    edge = jnp.pad(flux_xface[:, :, width - 1].T, ((0, 0), (0, LANES - rows_y)))
    seeds = jnp.asarray(seed_tables(half))
    bf16, f32, i16 = jnp.bfloat16, jnp.float32, jnp.int16
    vmem = pl.BlockSpec(memory_space=pltpu.VMEM)
    hbm = pl.BlockSpec(memory_space=pl.ANY)
    slab = (rows_y, depth, LANES)
    result = pl.pallas_call(
        functools.partial(kernel, gz, xy, chunks),
        out_shape=jax.ShapeDtypeStruct((tall, nz), f32),
        in_specs=[vmem, vmem, hbm, hbm, hbm, hbm],
        out_specs=vmem,
        scratch_shapes=[
            pltpu.VMEM(slab, bf16),
            pltpu.VMEM(slab, bf16),
            pltpu.VMEM(slab, bf16),
            pltpu.VMEM(seeds.shape, f32),
            pltpu.VMEM((depth, LANES), bf16),
            pltpu.VMEM(slab, i16),
            pltpu.VMEM((rows_y, 1, 2 * LANES), f32),
            pltpu.VMEM(slab, i16),
            pltpu.VMEM((rows_y, 1, 2 * LANES), f32),
            pltpu.VMEM((2, half, half), bf16),
            pltpu.VMEM((2, half, half), bf16),
            pltpu.VMEM((nz, 2 * LANES), bf16),
            pltpu.VMEM((half, 2 * LANES), bf16),
            pltpu.VMEM((half, 2 * LANES), bf16),
            pltpu.VMEM((xy, tall, LANES), i16),
            pltpu.VMEM((xy, 1, LANES), f32),
            pltpu.VMEM((xy, tall, LANES), i16),
            pltpu.VMEM((xy, 1, LANES), f32),
            pltpu.VMEM((2 * tall, nz), bf16),
            pltpu.VMEM((2 * tall, half), bf16),
            pltpu.VMEM((2 * tall, half), bf16),
            pltpu.VMEM((tall, nz), f32),
            pltpu.SemaphoreType.DMA((4,)),
            pltpu.SemaphoreType.DMA((2,)),
            pltpu.SemaphoreType.DMA((4,)),
            pltpu.SemaphoreType.DMA((4,)),
        ],
        compiler_params=pltpu.CompilerParams(
            collective_id=0, has_side_effects=True, vmem_limit_bytes=48 * 1024 * 1024
        ),
    )(weight, edge, seeds, flux_xface, flux_yspec, flux_zface)
    spread = result.reshape(2, tall // 2, 2, half).transpose(1, 0, 2, 3)
    return spread.reshape(1, tall, 2, half)


def solution(mesh):
    return jax.shard_map(
        functools.partial(shards, mesh.shape["gz"], mesh.shape["xy"]),
        mesh=mesh,
        in_specs=(P(None, "gz", "xy"), P(None, "gz", "xy"), P(None, "gz", "xy"), P()),
        out_specs=P("gz", "xy", None, None),
        check_vma=False,
    )
```

```python
import functools
import math

import jax
import jax.numpy as jnp
import numpy as np
from jax import lax
from jax.experimental import pallas as pl
from jax.experimental.pallas import tpu as pltpu
from jax.sharding import PartitionSpec as P

NY = 2048
SCREEN_WEIGHT = 0.5
MESH = pl.DeviceIdType.MESH
LANES = 128
ROWS = 16
STRIDE = 27
CODE_MAX = 32767.0
TINY = 1e-30


def seed_tables(half):
    period = 8 * half
    unit = 2.0 * np.pi / period
    row = np.arange(ROWS)[:, None]
    lane = np.arange(LANES)[None, :]
    phases = []
    for p in range(2):
        phases.append((2 * row + p) * (2 * lane + 1))
    block = np.arange(half // ROWS)[:, None]
    phases.append(2 * ROWS * block * (2 * lane + 1))
    for p in range(2):
        for a in range(half // LANES):
            phases.append((2 * row + p) * (2 * LANES * a) + 0 * lane)
    phase = np.concatenate(phases, axis=0) % period
    return np.stack([np.cos(phase * unit), np.sin(phase * unit)]).astype(np.float32)


def small_sine(angle):
    square = angle * angle
    total = jnp.full_like(angle, 1.0 / 6227020800.0)
    for divisor in (-39916800.0, 362880.0, -5040.0, 120.0, -6.0, 1.0):
        total = total * square + 1.0 / divisor
    return total * angle


def split(value):
    high = value.astype(jnp.bfloat16)
    return high, (value - high.astype(jnp.float32)).astype(jnp.bfloat16)


def coded(value, axis):
    largest = jnp.maximum(jnp.max(jnp.abs(value), axis=axis, keepdims=True), TINY)
    codes = jnp.round(value * (CODE_MAX / largest)).astype(jnp.int32)
    return codes.astype(jnp.int16), largest * (1.0 / CODE_MAX)


def mixed(a, b, transposed=False):
    dims = (((1,), (1,)), ((), ())) if transposed else (((1,), (0,)), ((), ()))
    return lax.dot_general(a, b, dims, preferred_element_type=jnp.float32)


def kernel(
    gz, xy, chunks, frequency_ref, seed_ref, fx_ref, fy_ref, fz_ref, out_ref,
    fx, fy, fz, seeds, weights, page, edge_out, edge_in, code1, side1, got1, gotside1, gotedge,
    table_hi, table_lo, planes, even, odd, code2, side2, got2, gotside2, factor, sums,
    load_sem, edge_sem, send1, recv1, send2, recv2,
):
    g = lax.axis_index("gz")
    r = lax.axis_index("xy")
    depth = fx_ref.shape[1]
    nz = gz * depth
    half = nz // 2
    turn = min(256, half)
    f32 = jnp.float32

    barrier = pltpu.get_barrier_semaphore()

    @pl.loop(1, gz, unroll=7)
    def _(i):
        peer = lax.rem(g + i * STRIDE, gz)
        pl.semaphore_signal(barrier, inc=1, device_id={"gz": peer}, device_id_type=MESH)

    for i in range(1, xy):
        peer = lax.rem(r + i, xy)
        pl.semaphore_signal(barrier, inc=1, device_id={"xy": peer}, device_id_type=MESH)

    loads = [
        pltpu.make_async_copy(src, dst, load_sem.at[i])
        for i, (src, dst) in enumerate(((fx_ref, fx), (fz_ref, fz), (fy_ref, fy), (seed_ref, seeds)))
    ]
    for load in loads:
        load.start()

    for y in range(gz):
        weights[y : y + 1, :] = jnp.full((1, LANES), frequency_ref[y].astype(f32))
    weights[...] = 2.0 * small_sine(weights[...] * (math.pi / (2 * NY)))

    for load in loads:
        load.wait()

    lane = lax.broadcasted_iota(jnp.int32, (depth, LANES), 1)
    plane = lax.broadcasted_iota(jnp.int32, (depth, LANES), 0)
    x_kept = (lane < LANES - 1) | (r < xy - 1)
    z_kept = (plane < depth - 1) | (g < gz - 1)

    def slab_of(y, edge):
        masked_x = jnp.where(x_kept, fx[y].astype(f32), 0.0)
        masked_z = jnp.where(z_kept, fz[y].astype(f32), 0.0)
        x_before = jnp.where(lane == 0, 0.0, pltpu.roll(masked_x, 1, 1))
        z_before = jnp.where(plane == 0, 0.0, pltpu.roll(masked_z, 1, 0))
        weight = weights[pl.ds(y, 1), :]
        slab = masked_x - x_before + weight * fy[y].astype(f32) + masked_z - z_before
        largest = jnp.maximum(jnp.max(jnp.abs(slab), axis=0, keepdims=True), TINY)
        scale = (largest * (1.01 / CODE_MAX)).astype(jnp.bfloat16).astype(f32)
        code1[y] = jnp.round(slab / scale).astype(jnp.int32).astype(jnp.int16)
        side1[y, 0:1, :] = scale.astype(jnp.bfloat16)
        side1[y, 1:2, :] = masked_z[depth - 1 :, :].astype(jnp.bfloat16)
        return jnp.where(lane == y, pltpu.roll(masked_x, lax.rem(y + 1, LANES), 1), edge)

    edge = lax.fori_loop(0, gz, slab_of, jnp.zeros((depth, LANES), f32), unroll=4)
    wide = jnp.concatenate([edge, jnp.zeros((LANES - depth, LANES), f32)], axis=0)
    page[...] = wide.T

    @pl.loop(0, gz, unroll=4)
    def _(y):
        edge_out[y] = page[pl.ds(y, 1), :]

    pl.semaphore_wait(barrier, gz + xy - 2)

    edge_copy = pltpu.make_async_remote_copy(
        src_ref=edge_out, dst_ref=edge_in, send_sem=edge_sem.at[0], recv_sem=edge_sem.at[1],
        device_id={"xy": lax.rem(r + 1, xy)}, device_id_type=MESH,
    )

    @pl.when(r < xy - 1)
    def _():
        edge_copy.start()

    def exchange1(source, target, which, peer):
        return pltpu.make_async_remote_copy(
            src_ref=source.at[peer], dst_ref=target.at[g], send_sem=send1.at[which], recv_sem=recv1.at[which],
            device_id={"gz": peer}, device_id_type=MESH,
        )

    @pl.loop(1, gz)
    def _(i):
        peer = lax.rem(g + i * STRIDE, gz)
        exchange1(code1, got1, 0, peer).start()
        exchange1(side1, gotside1, 1, peer).start()

    got1[g] = code1[g]
    gotside1[g] = side1[g]

    @pl.when(r > 0)
    def _():
        edge_copy.wait_recv()

        @pl.loop(1, gz)
        def _(i):
            exchange1(edge_in, gotedge, 2, lax.rem(g + i * STRIDE, gz)).start()

        gotedge[g] = edge_in[g]

    blocks = half // ROWS
    columns = half // LANES

    @pl.loop(0, blocks)
    def _(c):
        step_c = seeds[0, pl.ds(2 * ROWS + c, 1), :]
        step_s = seeds[1, pl.ds(2 * ROWS + c, 1), :]
        top = pl.multiple_of(c * ROWS, ROWS)
        for p in range(2):
            base_c = seeds[0, p * ROWS : (p + 1) * ROWS, :]
            base_s = seeds[1, p * ROWS : (p + 1) * ROWS, :]
            low_c = base_c * step_c - base_s * step_s
            low_s = base_s * step_c + base_c * step_s
            for a in range(columns):
                at = 2 * ROWS + blocks + (p * columns + a) * ROWS
                entry = seeds[0, at : at + ROWS, :] * low_c - seeds[1, at : at + ROWS, :] * low_s
                high, low = split(entry)
                table_hi[p, pl.ds(top, ROWS), a * LANES : (a + 1) * LANES] = high
                table_lo[p, pl.ds(top, ROWS), a * LANES : (a + 1) * LANES] = low

    across = lax.broadcasted_iota(jnp.int32, (turn, turn), 0) + lax.broadcasted_iota(jnp.int32, (turn, turn), 1)
    mirror = jnp.where(across == turn - 1, 1.0, 0.0).astype(jnp.bfloat16)

    rows = half // xy
    tall = 2 * rows
    unit = math.pi / (2 * nz)
    at_row = lax.broadcasted_iota(jnp.int32, (tall, LANES), 0)
    kz = tall * r + 2 * lax.rem(at_row, rows) + at_row // rows
    sine = small_sine(kz.astype(f32) * unit)
    weight = weights[pl.ds(g, 1), :]
    base = 4.0 * sine * sine + weight * weight + SCREEN_WEIGHT
    gain = jnp.where(kz == 0, -math.sqrt(0.5), -1.0) * (2.0 / nz)
    for p in range(2):
        for a in range(columns):
            kx = 2 * (lax.broadcasted_iota(jnp.int32, (1, LANES), 1) + a * LANES) + p
            sine = small_sine(kx.astype(f32) * unit)
            own = jnp.where(kx == 0, math.sqrt(0.5), 1.0)
            at = (p * columns + a) * LANES
            factor[:, at : at + LANES] = gain * own / (base + 4.0 * sine * sine)

    def all_but_one(ref, sem):
        part = ref.at[pl.ds(0, ref.shape[0] - 1)]
        return pltpu.make_async_copy(part, part, sem)

    @pl.when(r == 0)
    def _():
        gotedge[...] = jnp.zeros_like(gotedge)

    @pl.when(r > 0)
    def _():
        all_but_one(gotedge, recv1.at[2]).wait()

    page[...] = jnp.zeros_like(page)

    @pl.loop(0, gz, unroll=4)
    def _(k):
        page[pl.ds(k, 1), :] = gotedge[k]

    edges = page[...].T[:depth]

    all_but_one(gotside1, recv1.at[1]).wait()
    all_but_one(got1, recv1.at[0]).wait()

    @pl.loop(0, gz, unroll=2)
    def _(k):
        value = got1[k].astype(jnp.int32).astype(f32) * gotside1[k, 0:1, :].astype(f32)
        below = gotside1[jnp.maximum(k - 1, 0), 1:2, :].astype(f32)
        value = value - jnp.where((plane == 0) & (k > 0), below, 0.0)
        value = value - jnp.where(lane == 0, pltpu.roll(edges, lax.rem(LANES - k, LANES), 1), 0.0)
        high, low = split(value)
        at = pl.ds(pl.multiple_of(k * depth, depth), depth)
        planes[at, :LANES] = high
        planes[at, LANES:] = low

    for b in range(half // turn):
        here = slice(b * turn, (b + 1) * turn)
        there = slice(nz - (b + 1) * turn, nz - b * turn)
        lower = mixed(mirror, planes[there, :])
        lower = lower[:, :LANES] + lower[:, LANES:]
        upper = planes[here, :LANES].astype(f32) + planes[here, LANES:].astype(f32)
        even[here, :LANES], even[here, LANES:] = split(upper + lower)
        odd[here, :LANES], odd[here, LANES:] = split(upper - lower)

    def exchange2(source, target, which, peer):
        return pltpu.make_async_remote_copy(
            src_ref=source.at[peer], dst_ref=target.at[r], send_sem=send2.at[which], recv_sem=recv2.at[which, r],
            device_id={"xy": peer}, device_id_type=MESH,
        )

    chunk = half // chunks
    group = xy // chunks

    @pl.loop(0, chunks)
    def _(c):
        at_chunk = lax.rem(r // group + chunks // 2 + c, chunks)
        here = pl.ds(pl.multiple_of(at_chunk * chunk, chunk), chunk)
        parts = []
        for p, folded in enumerate((even, odd)):
            wide = mixed(table_hi[p, here, :], folded[...])
            narrow = mixed(table_lo[p, here, :], folded[:, :LANES])
            parts.append(wide[:, :LANES] + wide[:, LANES:] + narrow)
        for j in range(group):
            peer = at_chunk * group + j
            block = jnp.concatenate([part[j * rows : (j + 1) * rows] for part in parts], axis=0)
            codes, scale = coded(block, 0)
            code2[peer] = codes
            side2[peer] = scale

            @pl.when(peer != r)
            def _():
                exchange2(code2, got2, 0, peer).start()
                exchange2(side2, gotside2, 1, peer).start()

    got2[r] = code2[r]
    gotside2[r] = side2[r]

    pair = turn // LANES
    steps = half // turn

    def line_block(first):
        parts = []
        for i in range(pair):
            source = first + i

            @pl.when(source != r)
            def _():
                pltpu.make_async_copy(got2.at[source], got2.at[source], recv2.at[0, source]).wait()
                pltpu.make_async_copy(gotside2.at[source], gotside2.at[source], recv2.at[1, source]).wait()

            parts.append(got2[source].astype(jnp.int32).astype(f32) * gotside2[source])
        return jnp.concatenate(parts, axis=1)

    start = jnp.where(2 * r < xy, steps // 2, 0)
    for i in range(steps):
        b = lax.rem(start + i, steps)
        upper = line_block(b * pair)
        far = jnp.concatenate(split(line_block(xy - (b + 1) * pair)), axis=0)
        lower = mixed(far, mirror)
        lower = lower[:tall] + lower[tall:]
        here = pl.ds(pl.multiple_of(b * turn, turn), turn)
        for p, value in enumerate((upper + lower, upper - lower)):
            folded = jnp.concatenate(split(value), axis=0)
            for t in range(half // turn):
                entries = slice(t * turn, (t + 1) * turn)
                wide = mixed(folded, table_hi[p, entries, here], True)
                narrow = mixed(folded[:tall], table_lo[p, entries, here], True)
                total = wide[:tall] + wide[tall:] + narrow
                at = p * half + t * turn
                if i > 0:
                    total = total + sums[:, at : at + turn]
                if i < steps - 1:
                    sums[:, at : at + turn] = total
                    continue
                total = total * factor[:, at : at + turn]
                for z in range(2):
                    for a in range(pair):
                        row = z * 2 * columns + 2 * (t * pair + a) + p
                        out_ref[pl.ds(row, rows, stride=4 * columns), :] = total[
                            z * rows : (z + 1) * rows, a * LANES : (a + 1) * LANES
                        ]

    @pl.when(r < xy - 1)
    def _():
        edge_copy.wait_send()

    @pl.when(r > 0)
    def _():
        all_but_one(edge_in, send1.at[2]).wait()

    for ref, sem in ((code1, send1.at[0]), (side1, send1.at[1]), (code2, send2.at[0]), (side2, send2.at[1])):
        all_but_one(ref, sem).wait()


def shards(gz, xy, flux_xface, flux_yspec, flux_zface, frequency_y):
    rows_y, depth, width = flux_xface.shape
    nz = gz * depth
    half = nz // 2
    tall = nz // xy
    columns = half // LANES
    chunks = 4 if xy >= 8 else 2
    seeds = jnp.asarray(seed_tables(half))
    bf16, f32, i16 = jnp.bfloat16, jnp.float32, jnp.int16
    hbm = pl.BlockSpec(memory_space=pl.ANY)
    slab = (rows_y, depth, LANES)
    result = pl.pallas_call(
        functools.partial(kernel, gz, xy, chunks),
        out_shape=jax.ShapeDtypeStruct((tall * 2 * columns, LANES), f32),
        in_specs=[pl.BlockSpec(memory_space=pltpu.SMEM), hbm, hbm, hbm, hbm],
        out_specs=pl.BlockSpec(memory_space=pltpu.VMEM),
        scratch_shapes=[
            pltpu.VMEM(slab, bf16),
            pltpu.VMEM(slab, bf16),
            pltpu.VMEM(slab, bf16),
            pltpu.VMEM(seeds.shape, f32),
            pltpu.VMEM((rows_y, LANES), f32),
            pltpu.VMEM((LANES, LANES), f32),
            pltpu.VMEM((rows_y, 1, LANES), f32),
            pltpu.VMEM((rows_y, 1, LANES), f32),
            pltpu.VMEM(slab, i16),
            pltpu.VMEM((rows_y, 2, LANES), bf16),
            pltpu.VMEM(slab, i16),
            pltpu.VMEM((rows_y, 2, LANES), bf16),
            pltpu.VMEM((rows_y, 1, LANES), f32),
            pltpu.VMEM((2, half, half), bf16),
            pltpu.VMEM((2, half, half), bf16),
            pltpu.VMEM((nz, 2 * LANES), bf16),
            pltpu.VMEM((half, 2 * LANES), bf16),
            pltpu.VMEM((half, 2 * LANES), bf16),
            pltpu.VMEM((xy, tall, LANES), i16),
            pltpu.VMEM((xy, 1, LANES), f32),
            pltpu.VMEM((xy, tall, LANES), i16),
            pltpu.VMEM((xy, 1, LANES), f32),
            pltpu.VMEM((tall, nz), f32),
            pltpu.VMEM((tall, nz), f32),
            pltpu.SemaphoreType.DMA((4,)),
            pltpu.SemaphoreType.DMA((2,)),
            pltpu.SemaphoreType.DMA((3,)),
            pltpu.SemaphoreType.DMA((3,)),
            pltpu.SemaphoreType.DMA((2,)),
            pltpu.SemaphoreType.DMA((2, xy)),
        ],
        compiler_params=pltpu.CompilerParams(
            collective_id=0, has_side_effects=True, vmem_limit_bytes=60 * 1024 * 1024
        ),
    )(frequency_y, seeds, flux_xface, flux_yspec, flux_zface)
    spread = result.reshape(tall, columns, 2, LANES).transpose(0, 2, 1, 3)
    return spread.reshape(1, tall, 2, half)


def solution(mesh):
    return jax.shard_map(
        functools.partial(shards, mesh.shape["gz"], mesh.shape["xy"]),
        mesh=mesh,
        in_specs=(P(None, "gz", "xy"), P(None, "gz", "xy"), P(None, "gz", "xy"), P()),
        out_specs=P("gz", "xy", None, None),
        check_vma=False,
    )
```

```python
import functools
import math

import jax
import jax.numpy as jnp
import numpy as np
from jax import lax
from jax.experimental import pallas as pl
from jax.experimental.pallas import tpu as pltpu
from jax.sharding import PartitionSpec as P

NY = 2048
SCREEN_WEIGHT = 0.5
MESH = pl.DeviceIdType.MESH
LANES = 128
ROWS = 16
STRIDE = 27
CODE_MAX = 32767.0
TINY = 1e-30


def seed_tables(half):
    period = 8 * half
    unit = 2.0 * np.pi / period
    row = np.arange(ROWS)[:, None]
    lane = np.arange(LANES)[None, :]
    phases = []
    for p in range(2):
        phases.append((2 * row + p) * (2 * lane + 1))
    block = np.arange(half // ROWS)[:, None]
    phases.append(2 * ROWS * block * (2 * lane + 1))
    for p in range(2):
        for a in range(half // LANES):
            phases.append((2 * row + p) * (2 * LANES * a) + 0 * lane)
    phase = np.concatenate(phases, axis=0) % period
    return np.stack([np.cos(phase * unit), np.sin(phase * unit)]).astype(np.float32)


def small_sine(angle):
    square = angle * angle
    total = jnp.full_like(angle, 1.0 / 6227020800.0)
    for divisor in (-39916800.0, 362880.0, -5040.0, 120.0, -6.0, 1.0):
        total = total * square + 1.0 / divisor
    return total * angle


def split(value):
    high = value.astype(jnp.bfloat16)
    return high, (value - high.astype(jnp.float32)).astype(jnp.bfloat16)


def coded(value, axis):
    largest = jnp.maximum(jnp.max(jnp.abs(value), axis=axis, keepdims=True), TINY)
    codes = jnp.round(value * (CODE_MAX / largest)).astype(jnp.int32)
    return codes.astype(jnp.int16), largest * (1.0 / CODE_MAX)


def mixed(a, b, transposed=False):
    dims = (((1,), (1,)), ((), ())) if transposed else (((1,), (0,)), ((), ()))
    return lax.dot_general(a, b, dims, preferred_element_type=jnp.float32)


def kernel(
    gz, xy, chunks, frequency_ref, seed_ref, fx_ref, fy_ref, fz_ref, out_ref,
    fx, fy, fz, seeds, weights, page, edge_out, edge_in, code1, side1, got1, gotside1, gotedge,
    table_hi, table_lo, planes, even, odd, code2, side2, got2, gotside2, factor, sums,
    frequency, load_sem, edge_sem, send1, recv1, send2, recv2,
):
    g = lax.axis_index("gz")
    r = lax.axis_index("xy")
    depth = fx_ref.shape[1]
    nz = gz * depth
    half = nz // 2
    turn = min(256, half)
    f32 = jnp.float32

    loads = [
        pltpu.make_async_copy(src, dst, load_sem.at[i])
        for i, (src, dst) in enumerate(((frequency_ref, frequency), (fx_ref, fx), (fz_ref, fz), (fy_ref, fy), (seed_ref, seeds)))
    ]
    for load in loads:
        load.start()

    barrier = pltpu.get_barrier_semaphore()

    @pl.loop(1, gz, unroll=7)
    def _(i):
        peer = lax.rem(g + i * STRIDE, gz)
        pl.semaphore_signal(barrier, inc=1, device_id={"gz": peer}, device_id_type=MESH)

    for i in range(1, xy):
        peer = lax.rem(r + i, xy)
        pl.semaphore_signal(barrier, inc=1, device_id={"xy": peer}, device_id_type=MESH)

    loads[0].wait()
    for y in range(gz):
        weights[y : y + 1, :] = jnp.full((1, LANES), frequency[y].astype(f32))
    weights[...] = 2.0 * small_sine(weights[...] * (math.pi / (2 * NY)))

    for load in loads[1:4]:
        load.wait()

    lane = lax.broadcasted_iota(jnp.int32, (depth, LANES), 1)
    plane = lax.broadcasted_iota(jnp.int32, (depth, LANES), 0)
    x_kept = (lane < LANES - 1) | (r < xy - 1)
    z_kept = (plane < depth - 1) | (g < gz - 1)

    def slab_of(y, edge):
        masked_x = jnp.where(x_kept, fx[y].astype(f32), 0.0)
        masked_z = jnp.where(z_kept, fz[y].astype(f32), 0.0)
        x_before = jnp.where(lane == 0, 0.0, pltpu.roll(masked_x, 1, 1))
        z_before = jnp.where(plane == 0, 0.0, pltpu.roll(masked_z, 1, 0))
        weight = weights[pl.ds(y, 1), :]
        slab = masked_x - x_before + weight * fy[y].astype(f32) + masked_z - z_before
        largest = jnp.maximum(jnp.max(jnp.abs(slab), axis=0, keepdims=True), TINY)
        scale = (largest * (1.01 / CODE_MAX)).astype(jnp.bfloat16).astype(f32)
        code1[y] = jnp.round(slab * (1.0 / scale)).astype(jnp.int32).astype(jnp.int16)
        side1[y, 0:1, :] = scale.astype(jnp.bfloat16)
        side1[y, 1:2, :] = masked_z[depth - 1 :, :].astype(jnp.bfloat16)
        return jnp.where(lane == y, pltpu.roll(masked_x, lax.rem(y + 1, LANES), 1), edge)

    edge = lax.fori_loop(0, gz, slab_of, jnp.zeros((depth, LANES), f32), unroll=8)
    wide = jnp.concatenate([edge, jnp.zeros((LANES - depth, LANES), f32)], axis=0)
    page[...] = wide.T

    @pl.loop(0, gz, unroll=4)
    def _(y):
        edge_out[y] = page[pl.ds(y, 1), :]

    pl.semaphore_wait(barrier, gz + xy - 2)

    edge_copy = pltpu.make_async_remote_copy(
        src_ref=edge_out, dst_ref=edge_in, send_sem=edge_sem.at[0], recv_sem=edge_sem.at[1],
        device_id={"xy": lax.rem(r + 1, xy)}, device_id_type=MESH,
    )

    @pl.when(r < xy - 1)
    def _():
        edge_copy.start()

    def exchange1(source, target, which, peer):
        return pltpu.make_async_remote_copy(
            src_ref=source.at[peer], dst_ref=target.at[g], send_sem=send1.at[which], recv_sem=recv1.at[which],
            device_id={"gz": peer}, device_id_type=MESH,
        )

    @pl.loop(1, gz)
    def _(i):
        peer = lax.rem(g + i * STRIDE, gz)
        exchange1(code1, got1, 0, peer).start()
        exchange1(side1, gotside1, 1, peer).start()

    got1[g] = code1[g]
    gotside1[g] = side1[g]

    @pl.when(r > 0)
    def _():
        edge_copy.wait_recv()

        @pl.loop(1, gz)
        def _(i):
            exchange1(edge_in, gotedge, 2, lax.rem(g + i * STRIDE, gz)).start()

        gotedge[g] = edge_in[g]

    loads[4].wait()
    blocks = half // ROWS
    columns = half // LANES

    @pl.loop(0, blocks)
    def _(c):
        step_c = seeds[0, pl.ds(2 * ROWS + c, 1), :]
        step_s = seeds[1, pl.ds(2 * ROWS + c, 1), :]
        top = pl.multiple_of(c * ROWS, ROWS)
        for p in range(2):
            base_c = seeds[0, p * ROWS : (p + 1) * ROWS, :]
            base_s = seeds[1, p * ROWS : (p + 1) * ROWS, :]
            low_c = base_c * step_c - base_s * step_s
            low_s = base_s * step_c + base_c * step_s
            for a in range(columns):
                at = 2 * ROWS + blocks + (p * columns + a) * ROWS
                entry = seeds[0, at : at + ROWS, :] * low_c - seeds[1, at : at + ROWS, :] * low_s
                high, low = split(entry)
                table_hi[p, pl.ds(top, ROWS), a * LANES : (a + 1) * LANES] = high
                table_lo[p, pl.ds(top, ROWS), a * LANES : (a + 1) * LANES] = low

    across = lax.broadcasted_iota(jnp.int32, (turn, turn), 0) + lax.broadcasted_iota(jnp.int32, (turn, turn), 1)
    mirror = jnp.where(across == turn - 1, 1.0, 0.0).astype(jnp.bfloat16)

    rows = half // xy
    tall = 2 * rows
    unit = math.pi / (2 * nz)
    at_row = lax.broadcasted_iota(jnp.int32, (tall, LANES), 0)
    kz = tall * r + 2 * lax.rem(at_row, rows) + at_row // rows
    sine = small_sine(kz.astype(f32) * unit)
    weight = weights[pl.ds(g, 1), :]
    base = 4.0 * sine * sine + weight * weight + SCREEN_WEIGHT
    gain = jnp.where(kz == 0, -math.sqrt(0.5), -1.0) * (2.0 / nz)
    for p in range(2):
        for a in range(columns):
            kx = 2 * (lax.broadcasted_iota(jnp.int32, (1, LANES), 1) + a * LANES) + p
            sine = small_sine(kx.astype(f32) * unit)
            own = jnp.where(kx == 0, math.sqrt(0.5), 1.0)
            at = (p * columns + a) * LANES
            factor[:, at : at + LANES] = gain * own / (base + 4.0 * sine * sine)

    def all_but_one(ref, sem):
        part = ref.at[pl.ds(0, ref.shape[0] - 1)]
        return pltpu.make_async_copy(part, part, sem)

    @pl.when(r == 0)
    def _():
        gotedge[...] = jnp.zeros_like(gotedge)

    @pl.when(r > 0)
    def _():
        all_but_one(gotedge, recv1.at[2]).wait()

    page[...] = jnp.zeros_like(page)

    @pl.loop(0, gz, unroll=4)
    def _(k):
        page[pl.ds(k, 1), :] = gotedge[k]

    edges = page[...].T[:depth]

    all_but_one(gotside1, recv1.at[1]).wait()
    all_but_one(got1, recv1.at[0]).wait()

    @pl.loop(0, gz, unroll=8)
    def _(k):
        value = got1[k].astype(jnp.int32).astype(f32) * gotside1[k, 0:1, :].astype(f32)
        below = gotside1[jnp.maximum(k - 1, 0), 1:2, :].astype(f32)
        value = value - jnp.where((plane == 0) & (k > 0), below, 0.0)
        value = value - jnp.where(lane == 0, pltpu.roll(edges, lax.rem(LANES - k, LANES), 1), 0.0)
        high, low = split(value)
        at = pl.ds(pl.multiple_of(k * depth, depth), depth)
        planes[at, :LANES] = high
        planes[at, LANES:] = low

    for b in range(half // turn):
        here = slice(b * turn, (b + 1) * turn)
        there = slice(nz - (b + 1) * turn, nz - b * turn)
        lower = mixed(mirror, planes[there, :])
        lower = lower[:, :LANES] + lower[:, LANES:]
        upper = planes[here, :LANES].astype(f32) + planes[here, LANES:].astype(f32)
        even[here, :LANES], even[here, LANES:] = split(upper + lower)
        odd[here, :LANES], odd[here, LANES:] = split(upper - lower)

    def exchange2(source, target, which, peer):
        return pltpu.make_async_remote_copy(
            src_ref=source.at[peer], dst_ref=target.at[r], send_sem=send2.at[which], recv_sem=recv2.at[which, r],
            device_id={"xy": peer}, device_id_type=MESH,
        )

    chunk = half // chunks
    group = xy // chunks

    @pl.loop(0, chunks)
    def _(c):
        at_chunk = lax.rem(r // group + chunks // 2 + c, chunks)
        here = pl.ds(pl.multiple_of(at_chunk * chunk, chunk), chunk)
        parts = []
        for p, folded in enumerate((even, odd)):
            wide = mixed(table_hi[p, here, :], folded[...])
            narrow = mixed(table_lo[p, here, :], folded[:, :LANES])
            parts.append(wide[:, :LANES] + wide[:, LANES:] + narrow)
        for j in range(group):
            peer = at_chunk * group + j
            block = jnp.concatenate([part[j * rows : (j + 1) * rows] for part in parts], axis=0)
            codes, scale = coded(block, 0)
            code2[peer] = codes
            side2[peer] = scale
        for j in range(group):
            peer = at_chunk * group + lax.rem(r + j, group)

            @pl.when(peer != r)
            def _():
                exchange2(code2, got2, 0, peer).start()
                exchange2(side2, gotside2, 1, peer).start()

    got2[r] = code2[r]
    gotside2[r] = side2[r]

    pair = turn // LANES
    steps = half // turn

    def line_block(first):
        parts = []
        for i in range(pair):
            source = first + i

            @pl.when(source != r)
            def _():
                pltpu.make_async_copy(got2.at[source], got2.at[source], recv2.at[0, source]).wait()
                pltpu.make_async_copy(gotside2.at[source], gotside2.at[source], recv2.at[1, source]).wait()

            parts.append(got2[source].astype(jnp.int32).astype(f32) * gotside2[source])
        return jnp.concatenate(parts, axis=1)

    start = jnp.where(2 * r < xy, steps // 2, 0)
    for i in range(steps):
        b = lax.rem(start + i, steps)
        upper = line_block(b * pair)
        far = jnp.concatenate(split(line_block(xy - (b + 1) * pair)), axis=0)
        lower = mixed(far, mirror)
        lower = lower[:tall] + lower[tall:]
        here = pl.ds(pl.multiple_of(b * turn, turn), turn)
        for p, value in enumerate((upper + lower, upper - lower)):
            folded = jnp.concatenate(split(value), axis=0)
            for t in range(half // turn):
                entries = slice(t * turn, (t + 1) * turn)
                wide = mixed(folded, table_hi[p, entries, here], True)
                narrow = mixed(folded[:tall], table_lo[p, entries, here], True)
                total = wide[:tall] + wide[tall:] + narrow
                at = p * half + t * turn
                if i > 0:
                    total = total + sums[:, at : at + turn]
                if i < steps - 1:
                    sums[:, at : at + turn] = total
                    continue
                total = total * factor[:, at : at + turn]
                for z in range(2):
                    for a in range(pair):
                        row = z * 2 * columns + 2 * (t * pair + a) + p
                        out_ref[pl.ds(row, rows, stride=4 * columns), :] = total[
                            z * rows : (z + 1) * rows, a * LANES : (a + 1) * LANES
                        ]

    @pl.when(r < xy - 1)
    def _():
        edge_copy.wait_send()

    @pl.when(r > 0)
    def _():
        all_but_one(edge_in, send1.at[2]).wait()

    for ref, sem in ((code1, send1.at[0]), (side1, send1.at[1]), (code2, send2.at[0]), (side2, send2.at[1])):
        all_but_one(ref, sem).wait()


def put_out(held_ref, out_ref, sem):
    copy = pltpu.make_async_copy(held_ref, out_ref, sem)
    copy.start()
    copy.wait()


def shards(gz, xy, flux_xface, flux_yspec, flux_zface, frequency_y):
    rows_y, depth, width = flux_xface.shape
    nz = gz * depth
    half = nz // 2
    tall = nz // xy
    columns = half // LANES
    chunks = 4 if xy >= 8 else 2
    seeds = jnp.asarray(seed_tables(half))
    bf16, f32, i16 = jnp.bfloat16, jnp.float32, jnp.int16
    hbm = pl.BlockSpec(memory_space=pltpu.HBM)
    vmem = pl.BlockSpec(memory_space=pltpu.VMEM)
    slab = (rows_y, depth, LANES)
    result = pl.pallas_call(
        functools.partial(kernel, gz, xy, chunks),
        out_shape=jax.ShapeDtypeStruct((tall * 2 * columns, LANES), f32),
        in_specs=[hbm] * 5,
        out_specs=vmem,
        scratch_shapes=[
            pltpu.VMEM(slab, bf16),
            pltpu.VMEM(slab, bf16),
            pltpu.VMEM(slab, bf16),
            pltpu.VMEM(seeds.shape, f32),
            pltpu.VMEM((rows_y, LANES), f32),
            pltpu.VMEM((LANES, LANES), f32),
            pltpu.VMEM((rows_y, 1, LANES), f32),
            pltpu.VMEM((rows_y, 1, LANES), f32),
            pltpu.VMEM(slab, i16),
            pltpu.VMEM((rows_y, 2, LANES), bf16),
            pltpu.VMEM(slab, i16),
            pltpu.VMEM((rows_y, 2, LANES), bf16),
            pltpu.VMEM((rows_y, 1, LANES), f32),
            pltpu.VMEM((2, half, half), bf16),
            pltpu.VMEM((2, half, half), bf16),
            pltpu.VMEM((nz, 2 * LANES), bf16),
            pltpu.VMEM((half, 2 * LANES), bf16),
            pltpu.VMEM((half, 2 * LANES), bf16),
            pltpu.VMEM((xy, tall, LANES), i16),
            pltpu.VMEM((xy, 1, LANES), f32),
            pltpu.VMEM((xy, tall, LANES), i16),
            pltpu.VMEM((xy, 1, LANES), f32),
            pltpu.VMEM((tall, nz), f32),
            pltpu.VMEM((tall, nz), f32),
            pltpu.SMEM((rows_y,), jnp.int32),
            pltpu.SemaphoreType.DMA((5,)),
            pltpu.SemaphoreType.DMA((2,)),
            pltpu.SemaphoreType.DMA((3,)),
            pltpu.SemaphoreType.DMA((3,)),
            pltpu.SemaphoreType.DMA((2,)),
            pltpu.SemaphoreType.DMA((2, xy)),
        ],
        compiler_params=pltpu.CompilerParams(
            collective_id=0, has_side_effects=True, vmem_limit_bytes=24 * 1024 * 1024
        ),
    )(*(pltpu.with_memory_space_constraint(a, pltpu.HBM) for a in (frequency_y, seeds, flux_xface, flux_yspec, flux_zface)))
    result = pl.pallas_call(
        put_out,
        out_shape=jax.ShapeDtypeStruct(result.shape, f32),
        in_specs=[vmem],
        out_specs=hbm,
        scratch_shapes=[pltpu.SemaphoreType.DMA],
        compiler_params=pltpu.CompilerParams(vmem_limit_bytes=1024 * 1024),
    )(result)
    spread = result.reshape(tall, columns, 2, LANES).transpose(0, 2, 1, 3)
    return spread.reshape(1, tall, 2, half)


def solution(mesh):
    return jax.shard_map(
        functools.partial(shards, mesh.shape["gz"], mesh.shape["xy"]),
        mesh=mesh,
        in_specs=(P(None, "gz", "xy"), P(None, "gz", "xy"), P(None, "gz", "xy"), P()),
        out_specs=P("gz", "xy", None, None),
        check_vma=False,
    )
```

```python
import functools
import math

import jax
import jax.numpy as jnp
import numpy as np
from jax import lax
from jax.experimental import pallas as pl
from jax.experimental.pallas import tpu as pltpu
from jax.sharding import PartitionSpec as P

NY = 2048
SCREEN_WEIGHT = 0.5
MESH = pl.DeviceIdType.MESH
LANES = 128
ROWS = 16
STRIDE = 27
GROUP = 8
CODE_MAX = 32767.0
TINY = 1e-30


def seed_tables(half):
    period = 8 * half
    unit = 2.0 * np.pi / period
    row = np.arange(ROWS)[:, None]
    lane = np.arange(LANES)[None, :]
    phases = []
    for p in range(2):
        phases.append((2 * row + p) * (2 * lane + 1))
    block = np.arange(half // ROWS)[:, None]
    phases.append(2 * ROWS * block * (2 * lane + 1))
    for p in range(2):
        for a in range(half // LANES):
            phases.append((2 * row + p) * (2 * LANES * a) + 0 * lane)
    phase = np.concatenate(phases, axis=0) % period
    return np.stack([np.cos(phase * unit), np.sin(phase * unit)]).astype(np.float32)


def small_sine(angle):
    square = angle * angle
    total = jnp.full_like(angle, 1.0 / 6227020800.0)
    for divisor in (-39916800.0, 362880.0, -5040.0, 120.0, -6.0, 1.0):
        total = total * square + 1.0 / divisor
    return total * angle


def split(value):
    high = value.astype(jnp.bfloat16)
    return high, (value - high.astype(jnp.float32)).astype(jnp.bfloat16)


def coded(value, axis):
    largest = jnp.maximum(jnp.max(jnp.abs(value), axis=axis, keepdims=True), TINY)
    codes = jnp.round(value * (CODE_MAX / largest)).astype(jnp.int32)
    return codes.astype(jnp.int16), largest * (1.0 / CODE_MAX)


def mixed(a, b, transposed=False):
    dims = (((1,), (1,)), ((), ())) if transposed else (((1,), (0,)), ((), ()))
    return lax.dot_general(a, b, dims, preferred_element_type=jnp.float32)


def kernel(
    gz, xy, chunks, frequency_ref, seed_ref, fx_ref, fy_ref, fz_ref, out_ref,
    fx, fy, fz, seeds, weights, page, edge_out, edge_in, code1, side1, got1, gotside1, gotedge,
    table_hi, table_lo, even, odd, code2, side2, got2, gotside2, factor, sums,
    frequency, met_sem, load_sem, edge_sem, send1, recv1, send2, recv2,
):
    g = lax.axis_index("gz")
    r = lax.axis_index("xy")
    depth = fx_ref.shape[1]
    nz = gz * depth
    half = nz // 2
    turn = min(256, half)
    f32 = jnp.float32

    loads = [
        pltpu.make_async_copy(src, dst, load_sem.at[i])
        for i, (src, dst) in enumerate(((frequency_ref, frequency), (fx_ref, fx), (fz_ref, fz), (fy_ref, fy), (seed_ref, seeds)))
    ]
    for load in loads:
        load.start()

    barrier = pltpu.get_barrier_semaphore()

    @pl.loop(1, gz, unroll=7)
    def _(i):
        peer = lax.rem(g + i * STRIDE, gz)
        pl.semaphore_signal(barrier, inc=1, device_id={"gz": peer}, device_id_type=MESH)

    for i in range(1, xy):
        peer = lax.rem(r + i, xy)
        pl.semaphore_signal(barrier, inc=1, device_id={"gz": g - lax.rem(g, GROUP), "xy": peer}, device_id_type=MESH)

    loads[0].wait()
    for y in range(gz):
        weights[y : y + 1, :] = jnp.full((1, LANES), frequency[y].astype(f32))
    weights[...] = 2.0 * small_sine(weights[...] * (math.pi / (2 * NY)))

    for load in loads[1:4]:
        load.wait()

    lane = lax.broadcasted_iota(jnp.int32, (depth, LANES), 1)
    plane = lax.broadcasted_iota(jnp.int32, (depth, LANES), 0)
    x_kept = (lane < LANES - 1) | (r < xy - 1)
    z_kept = (plane < depth - 1) | (g < gz - 1)

    def slab_of(y, edge):
        masked_x = jnp.where(x_kept, fx[y].astype(f32), 0.0)
        masked_z = jnp.where(z_kept, fz[y].astype(f32), 0.0)
        x_before = jnp.where(lane == 0, 0.0, pltpu.roll(masked_x, 1, 1))
        z_before = jnp.where(plane == 0, 0.0, pltpu.roll(masked_z, 1, 0))
        weight = weights[pl.ds(y, 1), :]
        slab = masked_x - x_before + weight * fy[y].astype(f32) + masked_z - z_before
        largest = jnp.maximum(jnp.max(jnp.abs(slab), axis=0, keepdims=True), TINY)
        scale = (largest * (1.01 / CODE_MAX)).astype(jnp.bfloat16).astype(f32)
        code1[y] = jnp.round(slab * (1.0 / scale)).astype(jnp.int32).astype(jnp.int16)
        side1[y, 0:1, :] = scale.astype(jnp.bfloat16)
        side1[y, 1:2, :] = masked_z[depth - 1 :, :].astype(jnp.bfloat16)
        return jnp.where(lane == y, pltpu.roll(masked_x, lax.rem(y + 1, LANES), 1), edge)

    edge = lax.fori_loop(0, gz, slab_of, jnp.zeros((depth, LANES), f32), unroll=8)
    wide = jnp.concatenate([edge, jnp.zeros((LANES - depth, LANES), f32)], axis=0)
    page[...] = wide.T

    @pl.loop(0, gz, unroll=4)
    def _(y):
        edge_out[y] = page[pl.ds(y, 1), :]

    first = lax.rem(g, GROUP) == 0
    pl.semaphore_wait(barrier, gz - 1 + jnp.where(first, GROUP * (xy - 1), 0))

    @pl.when(first)
    def _():
        for i in range(1, GROUP):
            pl.semaphore_signal(met_sem, inc=1, device_id={"gz": g + i}, device_id_type=MESH)

    def exchange1(source, target, which, peer):
        return pltpu.make_async_remote_copy(
            src_ref=source.at[peer], dst_ref=target.at[g], send_sem=send1.at[which], recv_sem=recv1.at[which],
            device_id={"gz": peer}, device_id_type=MESH,
        )

    @pl.loop(1, gz)
    def _(i):
        peer = lax.rem(g + i * STRIDE, gz)
        exchange1(code1, got1, 0, peer).start()
        exchange1(side1, gotside1, 1, peer).start()

    got1[g] = code1[g]
    gotside1[g] = side1[g]

    loads[4].wait()
    blocks = half // ROWS
    columns = half // LANES

    @pl.loop(0, blocks)
    def _(c):
        step_c = seeds[0, pl.ds(2 * ROWS + c, 1), :]
        step_s = seeds[1, pl.ds(2 * ROWS + c, 1), :]
        top = pl.multiple_of(c * ROWS, ROWS)
        for p in range(2):
            base_c = seeds[0, p * ROWS : (p + 1) * ROWS, :]
            base_s = seeds[1, p * ROWS : (p + 1) * ROWS, :]
            low_c = base_c * step_c - base_s * step_s
            low_s = base_s * step_c + base_c * step_s
            for a in range(columns):
                at = 2 * ROWS + blocks + (p * columns + a) * ROWS
                entry = seeds[0, at : at + ROWS, :] * low_c - seeds[1, at : at + ROWS, :] * low_s
                high, low = split(entry)
                table_hi[p, pl.ds(top, ROWS), a * LANES : (a + 1) * LANES] = high
                table_lo[p, pl.ds(top, ROWS), a * LANES : (a + 1) * LANES] = low

    across = lax.broadcasted_iota(jnp.int32, (turn, turn), 0) + lax.broadcasted_iota(jnp.int32, (turn, turn), 1)
    mirror = jnp.where(across == turn - 1, 1.0, 0.0).astype(jnp.bfloat16)

    rows = half // xy
    tall = 2 * rows
    unit = math.pi / (2 * nz)
    at_row = lax.broadcasted_iota(jnp.int32, (tall, LANES), 0)
    kz = tall * r + 2 * lax.rem(at_row, rows) + at_row // rows
    sine = small_sine(kz.astype(f32) * unit)
    weight = weights[pl.ds(g, 1), :]
    base = 4.0 * sine * sine + weight * weight + SCREEN_WEIGHT
    gain = jnp.where(kz == 0, -math.sqrt(0.5), -1.0) * (2.0 / nz)
    for p in range(2):
        for a in range(columns):
            kx = 2 * (lax.broadcasted_iota(jnp.int32, (1, LANES), 1) + a * LANES) + p
            sine = small_sine(kx.astype(f32) * unit)
            own = jnp.where(kx == 0, math.sqrt(0.5), 1.0)
            at = (p * columns + a) * LANES
            factor[:, at : at + LANES] = gain * own / (base + 4.0 * sine * sine)

    @pl.when(jnp.logical_not(first))
    def _():
        pl.semaphore_wait(met_sem, 1)

    edge_copy = pltpu.make_async_remote_copy(
        src_ref=edge_out, dst_ref=edge_in, send_sem=edge_sem.at[0], recv_sem=edge_sem.at[1],
        device_id={"xy": lax.rem(r + 1, xy)}, device_id_type=MESH,
    )

    @pl.when(r < xy - 1)
    def _():
        edge_copy.start()

    @pl.when(r > 0)
    def _():
        edge_copy.wait_recv()

        @pl.loop(1, gz)
        def _(i):
            exchange1(edge_in, gotedge, 2, lax.rem(g + i * STRIDE, gz)).start()

        gotedge[g] = edge_in[g]

    def all_but_one(ref, sem):
        part = ref.at[pl.ds(0, ref.shape[0] - 1)]
        return pltpu.make_async_copy(part, part, sem)

    @pl.when(r == 0)
    def _():
        gotedge[...] = jnp.zeros_like(gotedge)

    @pl.when(r > 0)
    def _():
        all_but_one(gotedge, recv1.at[2]).wait()

    page[...] = jnp.zeros_like(page)

    @pl.loop(0, gz, unroll=4)
    def _(k):
        page[pl.ds(k, 1), :] = gotedge[k]

    edges = page[...].T[:depth]

    all_but_one(gotside1, recv1.at[1]).wait()
    all_but_one(got1, recv1.at[0]).wait()

    first_row = lax.broadcasted_iota(jnp.int32, (8, LANES), 0) == 0

    def decoded(k):
        side = gotside1[k].astype(f32)
        value = got1[k].astype(jnp.int32).astype(f32) * side[0:1]
        value = value - jnp.where(lane == 0, pltpu.roll(edges, (LANES - k) % LANES, 1), 0.0)
        if k == 0:
            return value
        below = gotside1[k - 1].astype(f32)[1:2]
        return jnp.concatenate([value[:8] - jnp.where(first_row, below, 0.0), value[8:]], axis=0)

    def plane_block(first):
        return jnp.concatenate([decoded(first // depth + i) for i in range(turn // depth)], axis=0)

    for b in range(half // turn):
        here = slice(b * turn, (b + 1) * turn)
        lower = mixed(mirror, jnp.concatenate(split(plane_block(nz - (b + 1) * turn)), axis=1))
        lower = lower[:, :LANES] + lower[:, LANES:]
        upper = plane_block(b * turn)
        even[here, :LANES], even[here, LANES:] = split(upper + lower)
        odd[here, :LANES], odd[here, LANES:] = split(upper - lower)

    def exchange2(source, target, which, peer):
        return pltpu.make_async_remote_copy(
            src_ref=source.at[peer], dst_ref=target.at[r], send_sem=send2.at[which], recv_sem=recv2.at[which, r],
            device_id={"xy": peer}, device_id_type=MESH,
        )

    chunk = half // chunks
    group = xy // chunks
    wings = chunks // 2

    @pl.loop(0, chunks)
    def _(c):
        side = lax.rem(r // (xy // 2) + 1 + c, 2)
        along = lax.rem(lax.rem(r // group, wings) + wings // 2 + c // 2, wings)
        at_chunk = side * wings + along
        here = pl.ds(pl.multiple_of(at_chunk * chunk, chunk), chunk)
        parts = []
        for p, folded in enumerate((even, odd)):
            wide = mixed(table_hi[p, here, :], folded[...])
            narrow = mixed(table_lo[p, here, :], folded[:, :LANES])
            parts.append(wide[:, :LANES] + wide[:, LANES:] + narrow)
        for j in range(group):
            peer = at_chunk * group + j
            block = jnp.concatenate([part[j * rows : (j + 1) * rows] for part in parts], axis=0)
            codes, scale = coded(block, 0)
            code2[peer] = codes
            side2[peer] = scale
        for j in range(group):
            peer = at_chunk * group + lax.rem(r + j, group)

            @pl.when(peer != r)
            def _():
                exchange2(code2, got2, 0, peer).start()
                exchange2(side2, gotside2, 1, peer).start()

    got2[r] = code2[r]
    gotside2[r] = side2[r]

    pair = turn // LANES
    steps = half // turn

    def line_block(first):
        parts = []
        for i in range(pair):
            source = first + i

            @pl.when(source != r)
            def _():
                pltpu.make_async_copy(got2.at[source], got2.at[source], recv2.at[0, source]).wait()
                pltpu.make_async_copy(gotside2.at[source], gotside2.at[source], recv2.at[1, source]).wait()

            parts.append(got2[source].astype(jnp.int32).astype(f32) * gotside2[source])
        return jnp.concatenate(parts, axis=1)

    start = jnp.where(4 * lax.rem(r, xy // 2) < xy, 1, steps - 1)
    for i in range(steps):
        b = lax.rem(start + i, steps)
        upper = line_block(b * pair)
        far = jnp.concatenate(split(line_block(xy - (b + 1) * pair)), axis=0)
        lower = mixed(far, mirror)
        lower = lower[:tall] + lower[tall:]
        here = pl.ds(pl.multiple_of(b * turn, turn), turn)
        for p, value in enumerate((upper + lower, upper - lower)):
            folded = jnp.concatenate(split(value), axis=0)
            for t in range(half // turn):
                entries = slice(t * turn, (t + 1) * turn)
                wide = mixed(folded, table_hi[p, entries, here], True)
                narrow = mixed(folded[:tall], table_lo[p, entries, here], True)
                total = wide[:tall] + wide[tall:] + narrow
                at = p * half + t * turn
                if i > 0:
                    total = total + sums[:, at : at + turn]
                if i < steps - 1:
                    sums[:, at : at + turn] = total
                    continue
                total = total * factor[:, at : at + turn]
                for z in range(2):
                    for a in range(pair):
                        row = z * 2 * columns + 2 * (t * pair + a) + p
                        out_ref[pl.ds(row, rows, stride=4 * columns), :] = total[
                            z * rows : (z + 1) * rows, a * LANES : (a + 1) * LANES
                        ]

    @pl.when(r < xy - 1)
    def _():
        edge_copy.wait_send()

    @pl.when(r > 0)
    def _():
        all_but_one(edge_in, send1.at[2]).wait()

    for ref, sem in ((code1, send1.at[0]), (side1, send1.at[1]), (code2, send2.at[0]), (side2, send2.at[1])):
        all_but_one(ref, sem).wait()


def put_out(held_ref, out_ref, sem):
    copy = pltpu.make_async_copy(held_ref, out_ref, sem)
    copy.start()
    copy.wait()


def shards(gz, xy, flux_xface, flux_yspec, flux_zface, frequency_y):
    rows_y, depth, width = flux_xface.shape
    nz = gz * depth
    half = nz // 2
    tall = nz // xy
    columns = half // LANES
    chunks = 4 if xy >= 8 else 2
    seeds = jnp.asarray(seed_tables(half))
    bf16, f32, i16 = jnp.bfloat16, jnp.float32, jnp.int16
    hbm = pl.BlockSpec(memory_space=pltpu.HBM)
    vmem = pl.BlockSpec(memory_space=pltpu.VMEM)
    slab = (rows_y, depth, LANES)
    result = pl.pallas_call(
        functools.partial(kernel, gz, xy, chunks),
        out_shape=jax.ShapeDtypeStruct((tall * 2 * columns, LANES), f32),
        in_specs=[hbm] * 5,
        out_specs=vmem,
        scratch_shapes=[
            pltpu.VMEM(slab, bf16),
            pltpu.VMEM(slab, bf16),
            pltpu.VMEM(slab, bf16),
            pltpu.VMEM(seeds.shape, f32),
            pltpu.VMEM((rows_y, LANES), f32),
            pltpu.VMEM((LANES, LANES), f32),
            pltpu.VMEM((rows_y, 1, LANES), f32),
            pltpu.VMEM((rows_y, 1, LANES), f32),
            pltpu.VMEM(slab, i16),
            pltpu.VMEM((rows_y, 2, LANES), bf16),
            pltpu.VMEM(slab, i16),
            pltpu.VMEM((rows_y, 2, LANES), bf16),
            pltpu.VMEM((rows_y, 1, LANES), f32),
            pltpu.VMEM((2, half, half), bf16),
            pltpu.VMEM((2, half, half), bf16),
            pltpu.VMEM((half, 2 * LANES), bf16),
            pltpu.VMEM((half, 2 * LANES), bf16),
            pltpu.VMEM((xy, tall, LANES), i16),
            pltpu.VMEM((xy, 1, LANES), f32),
            pltpu.VMEM((xy, tall, LANES), i16),
            pltpu.VMEM((xy, 1, LANES), f32),
            pltpu.VMEM((tall, nz), f32),
            pltpu.VMEM((tall, nz), f32),
            pltpu.SMEM((rows_y,), jnp.int32),
            pltpu.SemaphoreType.REGULAR,
            pltpu.SemaphoreType.DMA((5,)),
            pltpu.SemaphoreType.DMA((2,)),
            pltpu.SemaphoreType.DMA((3,)),
            pltpu.SemaphoreType.DMA((3,)),
            pltpu.SemaphoreType.DMA((2,)),
            pltpu.SemaphoreType.DMA((2, xy)),
        ],
        compiler_params=pltpu.CompilerParams(
            collective_id=0, has_side_effects=True, vmem_limit_bytes=24 * 1024 * 1024
        ),
    )(*(pltpu.with_memory_space_constraint(a, pltpu.HBM) for a in (frequency_y, seeds, flux_xface, flux_yspec, flux_zface)))
    result = pl.pallas_call(
        put_out,
        out_shape=jax.ShapeDtypeStruct(result.shape, f32),
        in_specs=[vmem],
        out_specs=hbm,
        scratch_shapes=[pltpu.SemaphoreType.DMA],
        compiler_params=pltpu.CompilerParams(vmem_limit_bytes=1024 * 1024),
    )(result)
    spread = result.reshape(tall, columns, 2, LANES).transpose(0, 2, 1, 3)
    return spread.reshape(1, tall, 2, half)


def solution(mesh):
    return jax.shard_map(
        functools.partial(shards, mesh.shape["gz"], mesh.shape["xy"]),
        mesh=mesh,
        in_specs=(P(None, "gz", "xy"), P(None, "gz", "xy"), P(None, "gz", "xy"), P()),
        out_specs=P("gz", "xy", None, None),
        check_vma=False,
    )
```

```python
import functools
import math

import jax
import jax.numpy as jnp
import numpy as np
from jax import lax
from jax.experimental import pallas as pl
from jax.experimental.pallas import tpu as pltpu
from jax.sharding import PartitionSpec as P

NY = 2048
SCREEN_WEIGHT = 0.5
MESH = pl.DeviceIdType.MESH
LANES = 128
ROWS = 16
STRIDE = 27
GROUP = 4
CODE_MAX = 32767.0
TINY = 1e-30


def seed_tables(half):
    period = 8 * half
    unit = 2.0 * np.pi / period
    row = np.arange(ROWS)[:, None]
    lane = np.arange(LANES)[None, :]
    phases = []
    for p in range(2):
        phases.append((2 * row + p) * (2 * lane + 1))
    block = np.arange(half // ROWS)[:, None]
    phases.append(2 * ROWS * block * (2 * lane + 1))
    for p in range(2):
        for a in range(half // LANES):
            phases.append((2 * row + p) * (2 * LANES * a) + 0 * lane)
    phase = np.concatenate(phases, axis=0) % period
    return np.stack([np.cos(phase * unit), np.sin(phase * unit)]).astype(np.float32)


def small_sine(angle):
    square = angle * angle
    total = jnp.full_like(angle, 1.0 / 6227020800.0)
    for divisor in (-39916800.0, 362880.0, -5040.0, 120.0, -6.0, 1.0):
        total = total * square + 1.0 / divisor
    return total * angle


def split(value):
    high = value.astype(jnp.bfloat16)
    return high, (value - high.astype(jnp.float32)).astype(jnp.bfloat16)


def coded(value, axis):
    largest = jnp.maximum(jnp.max(jnp.abs(value), axis=axis, keepdims=True), TINY)
    codes = jnp.round(value * (CODE_MAX / largest)).astype(jnp.int32)
    return codes.astype(jnp.int16), largest * (1.0 / CODE_MAX)


def mixed(a, b, transposed=False):
    dims = (((1,), (1,)), ((), ())) if transposed else (((1,), (0,)), ((), ()))
    return lax.dot_general(a, b, dims, preferred_element_type=jnp.float32)


def kernel(
    gz, xy, chunks, frequency_ref, seed_ref, fx_ref, fy_ref, fz_ref, out_ref,
    fx, fy, fz, seeds, weights, page, edge_out, edge_in, code1, side1, got1, gotside1, gotedge,
    table_hi, table_lo, even, odd, code2, side2, got2, gotside2, factor, sums,
    frequency, met_sem, load_sem, edge_sem, send1, recv1, send2, recv2,
):
    g = lax.axis_index("gz")
    r = lax.axis_index("xy")
    depth = fx_ref.shape[1]
    nz = gz * depth
    half = nz // 2
    turn = min(256, half)
    f32 = jnp.float32

    loads = [
        pltpu.make_async_copy(src, dst, load_sem.at[i])
        for i, (src, dst) in enumerate(((frequency_ref, frequency), (fx_ref, fx), (fz_ref, fz), (fy_ref, fy), (seed_ref, seeds)))
    ]
    for load in loads:
        load.start()

    barrier = pltpu.get_barrier_semaphore()

    @pl.loop(1, gz, unroll=7)
    def _(i):
        peer = lax.rem(g + i * STRIDE, gz)
        pl.semaphore_signal(barrier, inc=1, device_id={"gz": peer}, device_id_type=MESH)

    for i in range(1, xy):
        peer = lax.rem(r + i, xy)
        pl.semaphore_signal(barrier, inc=1, device_id={"gz": g - lax.rem(g, GROUP), "xy": peer}, device_id_type=MESH)

    loads[0].wait()
    for y in range(gz):
        weights[y : y + 1, :] = jnp.full((1, LANES), frequency[y].astype(f32))
    weights[...] = 2.0 * small_sine(weights[...] * (math.pi / (2 * NY)))

    for load in loads[1:4]:
        load.wait()

    lane = lax.broadcasted_iota(jnp.int32, (depth, LANES), 1)
    plane = lax.broadcasted_iota(jnp.int32, (depth, LANES), 0)
    x_kept = (lane < LANES - 1) | (r < xy - 1)
    z_kept = (plane < depth - 1) | (g < gz - 1)

    def slab_of(y, edge):
        masked_x = jnp.where(x_kept, fx[y].astype(f32), 0.0)
        masked_z = jnp.where(z_kept, fz[y].astype(f32), 0.0)
        x_before = jnp.where(lane == 0, 0.0, pltpu.roll(masked_x, 1, 1))
        z_before = jnp.where(plane == 0, 0.0, pltpu.roll(masked_z, 1, 0))
        weight = weights[pl.ds(y, 1), :]
        slab = masked_x - x_before + weight * fy[y].astype(f32) + masked_z - z_before
        largest = jnp.maximum(jnp.max(jnp.abs(slab), axis=0, keepdims=True), TINY)
        scale = (largest * (1.01 / CODE_MAX)).astype(jnp.bfloat16).astype(f32)
        code1[y] = jnp.round(slab * (1.0 / scale)).astype(jnp.int32).astype(jnp.int16)
        side1[y, 0:1, :] = scale.astype(jnp.bfloat16)
        side1[y, 1:2, :] = masked_z[depth - 1 :, :].astype(jnp.bfloat16)
        return jnp.where(lane == y, pltpu.roll(masked_x, lax.rem(y + 1, LANES), 1), edge)

    edge = lax.fori_loop(0, gz, slab_of, jnp.zeros((depth, LANES), f32), unroll=8)
    wide = jnp.concatenate([edge, jnp.zeros((LANES - depth, LANES), f32)], axis=0)
    page[...] = wide.T

    @pl.loop(0, gz, unroll=4)
    def _(y):
        edge_out[y] = page[pl.ds(y, 1), :]

    first = lax.rem(g, GROUP) == 0
    pl.semaphore_wait(barrier, gz - 1 + jnp.where(first, GROUP * (xy - 1), 0))

    @pl.when(first)
    def _():
        for i in range(1, GROUP):
            pl.semaphore_signal(met_sem, inc=1, device_id={"gz": g + i}, device_id_type=MESH)

    def exchange1(source, target, which, peer):
        return pltpu.make_async_remote_copy(
            src_ref=source.at[peer], dst_ref=target.at[g], send_sem=send1.at[which], recv_sem=recv1.at[which],
            device_id={"gz": peer}, device_id_type=MESH,
        )

    @pl.loop(1, gz)
    def _(i):
        peer = lax.rem(g + i * STRIDE, gz)
        exchange1(code1, got1, 0, peer).start()
        exchange1(side1, gotside1, 1, peer).start()

    got1[g] = code1[g]
    gotside1[g] = side1[g]

    @pl.when(jnp.logical_not(first))
    def _():
        pl.semaphore_wait(met_sem, 1)

    edge_copy = pltpu.make_async_remote_copy(
        src_ref=edge_out, dst_ref=edge_in, send_sem=edge_sem.at[0], recv_sem=edge_sem.at[1],
        device_id={"xy": lax.rem(r + 1, xy)}, device_id_type=MESH,
    )

    @pl.when(r < xy - 1)
    def _():
        edge_copy.start()

    loads[4].wait()
    blocks = half // ROWS
    columns = half // LANES

    @pl.loop(0, blocks)
    def _(c):
        step_c = seeds[0, pl.ds(2 * ROWS + c, 1), :]
        step_s = seeds[1, pl.ds(2 * ROWS + c, 1), :]
        top = pl.multiple_of(c * ROWS, ROWS)
        for p in range(2):
            base_c = seeds[0, p * ROWS : (p + 1) * ROWS, :]
            base_s = seeds[1, p * ROWS : (p + 1) * ROWS, :]
            low_c = base_c * step_c - base_s * step_s
            low_s = base_s * step_c + base_c * step_s
            for a in range(columns):
                at = 2 * ROWS + blocks + (p * columns + a) * ROWS
                entry = seeds[0, at : at + ROWS, :] * low_c - seeds[1, at : at + ROWS, :] * low_s
                high, low = split(entry)
                table_hi[p, pl.ds(top, ROWS), a * LANES : (a + 1) * LANES] = high
                table_lo[p, pl.ds(top, ROWS), a * LANES : (a + 1) * LANES] = low

    across = lax.broadcasted_iota(jnp.int32, (turn, turn), 0) + lax.broadcasted_iota(jnp.int32, (turn, turn), 1)
    mirror = jnp.where(across == turn - 1, 1.0, 0.0).astype(jnp.bfloat16)

    rows = half // xy
    tall = 2 * rows
    unit = math.pi / (2 * nz)
    at_row = lax.broadcasted_iota(jnp.int32, (tall, LANES), 0)
    kz = tall * r + 2 * lax.rem(at_row, rows) + at_row // rows
    sine = small_sine(kz.astype(f32) * unit)
    weight = weights[pl.ds(g, 1), :]
    base = 4.0 * sine * sine + weight * weight + SCREEN_WEIGHT
    gain = jnp.where(kz == 0, -math.sqrt(0.5), -1.0) * (2.0 / nz)
    for p in range(2):
        for a in range(columns):
            kx = 2 * (lax.broadcasted_iota(jnp.int32, (1, LANES), 1) + a * LANES) + p
            sine = small_sine(kx.astype(f32) * unit)
            own = jnp.where(kx == 0, math.sqrt(0.5), 1.0)
            at = (p * columns + a) * LANES
            factor[:, at : at + LANES] = gain * own / (base + 4.0 * sine * sine)

    @pl.when(r > 0)
    def _():
        edge_copy.wait_recv()

        @pl.loop(1, gz)
        def _(i):
            exchange1(edge_in, gotedge, 2, lax.rem(g + i * STRIDE, gz)).start()

        gotedge[g] = edge_in[g]

    def all_but_one(ref, sem):
        part = ref.at[pl.ds(0, ref.shape[0] - 1)]
        return pltpu.make_async_copy(part, part, sem)

    @pl.when(r == 0)
    def _():
        gotedge[...] = jnp.zeros_like(gotedge)

    @pl.when(r > 0)
    def _():
        all_but_one(gotedge, recv1.at[2]).wait()

    page[...] = jnp.zeros_like(page)

    @pl.loop(0, gz, unroll=4)
    def _(k):
        page[pl.ds(k, 1), :] = gotedge[k]

    edges = page[...].T[:depth]

    all_but_one(gotside1, recv1.at[1]).wait()
    all_but_one(got1, recv1.at[0]).wait()

    first_row = lax.broadcasted_iota(jnp.int32, (8, LANES), 0) == 0

    def decoded(k):
        side = gotside1[k].astype(f32)
        value = got1[k].astype(jnp.int32).astype(f32) * side[0:1]
        value = value - jnp.where(lane == 0, pltpu.roll(edges, (LANES - k) % LANES, 1), 0.0)
        if k == 0:
            return value
        below = gotside1[k - 1].astype(f32)[1:2]
        return jnp.concatenate([value[:8] - jnp.where(first_row, below, 0.0), value[8:]], axis=0)

    def plane_block(first):
        return jnp.concatenate([decoded(first // depth + i) for i in range(turn // depth)], axis=0)

    for b in range(half // turn):
        here = slice(b * turn, (b + 1) * turn)
        lower = mixed(mirror, jnp.concatenate(split(plane_block(nz - (b + 1) * turn)), axis=1))
        lower = lower[:, :LANES] + lower[:, LANES:]
        upper = plane_block(b * turn)
        even[here, :LANES], even[here, LANES:] = split(upper + lower)
        odd[here, :LANES], odd[here, LANES:] = split(upper - lower)

    def exchange2(source, target, which, peer):
        return pltpu.make_async_remote_copy(
            src_ref=source.at[peer], dst_ref=target.at[r], send_sem=send2.at[which], recv_sem=recv2.at[which, r],
            device_id={"xy": peer}, device_id_type=MESH,
        )

    chunk = half // chunks
    group = xy // chunks
    wings = chunks // 2

    @pl.loop(0, chunks)
    def _(c):
        side = lax.rem(r // (xy // 2) + 1 + c, 2)
        along = lax.rem(lax.rem(r // group, wings) + wings // 2 + c // 2, wings)
        at_chunk = side * wings + along
        here = pl.ds(pl.multiple_of(at_chunk * chunk, chunk), chunk)
        parts = []
        for p, folded in enumerate((even, odd)):
            wide = mixed(table_hi[p, here, :], folded[...])
            narrow = mixed(table_lo[p, here, :], folded[:, :LANES])
            parts.append(wide[:, :LANES] + wide[:, LANES:] + narrow)
        for j in range(group):
            peer = at_chunk * group + j
            block = jnp.concatenate([part[j * rows : (j + 1) * rows] for part in parts], axis=0)
            codes, scale = coded(block, 0)
            code2[peer] = codes
            side2[peer] = scale
        for j in range(group):
            peer = at_chunk * group + lax.rem(r + j, group)

            @pl.when(peer != r)
            def _():
                exchange2(code2, got2, 0, peer).start()
                exchange2(side2, gotside2, 1, peer).start()

    got2[r] = code2[r]
    gotside2[r] = side2[r]

    pair = turn // LANES
    steps = half // turn

    def line_block(first):
        parts = []
        for i in range(pair):
            source = first + i

            @pl.when(source != r)
            def _():
                pltpu.make_async_copy(got2.at[source], got2.at[source], recv2.at[0, source]).wait()
                pltpu.make_async_copy(gotside2.at[source], gotside2.at[source], recv2.at[1, source]).wait()

            parts.append(got2[source].astype(jnp.int32).astype(f32) * gotside2[source])
        return jnp.concatenate(parts, axis=1)

    start = jnp.where(4 * lax.rem(r, xy // 2) < xy, 1, steps - 1)
    for i in range(steps):
        b = lax.rem(start + i, steps)
        upper = line_block(b * pair)
        far = jnp.concatenate(split(line_block(xy - (b + 1) * pair)), axis=0)
        lower = mixed(far, mirror)
        lower = lower[:tall] + lower[tall:]
        here = pl.ds(pl.multiple_of(b * turn, turn), turn)
        for p, value in enumerate((upper + lower, upper - lower)):
            folded = jnp.concatenate(split(value), axis=0)
            for t in range(half // turn):
                entries = slice(t * turn, (t + 1) * turn)
                wide = mixed(folded, table_hi[p, entries, here], True)
                narrow = mixed(folded[:tall], table_lo[p, entries, here], True)
                total = wide[:tall] + wide[tall:] + narrow
                at = p * half + t * turn
                if i > 0:
                    total = total + sums[:, at : at + turn]
                if i < steps - 1:
                    sums[:, at : at + turn] = total
                    continue
                total = total * factor[:, at : at + turn]
                for z in range(2):
                    for a in range(pair):
                        row = z * 2 * columns + 2 * (t * pair + a) + p
                        out_ref[pl.ds(row, rows, stride=4 * columns), :] = total[
                            z * rows : (z + 1) * rows, a * LANES : (a + 1) * LANES
                        ]

    @pl.when(r < xy - 1)
    def _():
        edge_copy.wait_send()

    @pl.when(r > 0)
    def _():
        all_but_one(edge_in, send1.at[2]).wait()

    for ref, sem in ((code1, send1.at[0]), (side1, send1.at[1]), (code2, send2.at[0]), (side2, send2.at[1])):
        all_but_one(ref, sem).wait()


def put_out(held_ref, out_ref, sem):
    copy = pltpu.make_async_copy(held_ref, out_ref, sem)
    copy.start()
    copy.wait()


def shards(gz, xy, flux_xface, flux_yspec, flux_zface, frequency_y):
    rows_y, depth, width = flux_xface.shape
    nz = gz * depth
    half = nz // 2
    tall = nz // xy
    columns = half // LANES
    chunks = 4 if xy >= 8 else 2
    seeds = jnp.asarray(seed_tables(half))
    bf16, f32, i16 = jnp.bfloat16, jnp.float32, jnp.int16
    hbm = pl.BlockSpec(memory_space=pltpu.HBM)
    vmem = pl.BlockSpec(memory_space=pltpu.VMEM)
    slab = (rows_y, depth, LANES)
    result = pl.pallas_call(
        functools.partial(kernel, gz, xy, chunks),
        out_shape=jax.ShapeDtypeStruct((tall * 2 * columns, LANES), f32),
        in_specs=[hbm] * 5,
        out_specs=vmem,
        scratch_shapes=[
            pltpu.VMEM(slab, bf16),
            pltpu.VMEM(slab, bf16),
            pltpu.VMEM(slab, bf16),
            pltpu.VMEM(seeds.shape, f32),
            pltpu.VMEM((rows_y, LANES), f32),
            pltpu.VMEM((LANES, LANES), f32),
            pltpu.VMEM((rows_y, 1, LANES), f32),
            pltpu.VMEM((rows_y, 1, LANES), f32),
            pltpu.VMEM(slab, i16),
            pltpu.VMEM((rows_y, 2, LANES), bf16),
            pltpu.VMEM(slab, i16),
            pltpu.VMEM((rows_y, 2, LANES), bf16),
            pltpu.VMEM((rows_y, 1, LANES), f32),
            pltpu.VMEM((2, half, half), bf16),
            pltpu.VMEM((2, half, half), bf16),
            pltpu.VMEM((half, 2 * LANES), bf16),
            pltpu.VMEM((half, 2 * LANES), bf16),
            pltpu.VMEM((xy, tall, LANES), i16),
            pltpu.VMEM((xy, 1, LANES), f32),
            pltpu.VMEM((xy, tall, LANES), i16),
            pltpu.VMEM((xy, 1, LANES), f32),
            pltpu.VMEM((tall, nz), f32),
            pltpu.VMEM((tall, nz), f32),
            pltpu.SMEM((rows_y,), jnp.int32),
            pltpu.SemaphoreType.REGULAR,
            pltpu.SemaphoreType.DMA((5,)),
            pltpu.SemaphoreType.DMA((2,)),
            pltpu.SemaphoreType.DMA((3,)),
            pltpu.SemaphoreType.DMA((3,)),
            pltpu.SemaphoreType.DMA((2,)),
            pltpu.SemaphoreType.DMA((2, xy)),
        ],
        compiler_params=pltpu.CompilerParams(
            collective_id=0, has_side_effects=True, vmem_limit_bytes=24 * 1024 * 1024
        ),
    )(*(pltpu.with_memory_space_constraint(a, pltpu.HBM) for a in (frequency_y, seeds, flux_xface, flux_yspec, flux_zface)))
    result = pl.pallas_call(
        put_out,
        out_shape=jax.ShapeDtypeStruct(result.shape, f32),
        in_specs=[vmem],
        out_specs=hbm,
        scratch_shapes=[pltpu.SemaphoreType.DMA],
        compiler_params=pltpu.CompilerParams(vmem_limit_bytes=1024 * 1024),
    )(result)
    spread = result.reshape(tall, columns, 2, LANES).transpose(0, 2, 1, 3)
    return spread.reshape(1, tall, 2, half)


def solution(mesh):
    return jax.shard_map(
        functools.partial(shards, mesh.shape["gz"], mesh.shape["xy"]),
        mesh=mesh,
        in_specs=(P(None, "gz", "xy"), P(None, "gz", "xy"), P(None, "gz", "xy"), P()),
        out_specs=P("gz", "xy", None, None),
        check_vma=False,
    )
```
